32 devices in a mesh: shard: 4 (over z), tensor: 4 (over x, core), section: 2 (over y).
Axes of the slice: x: 2, y: 2, z: 4, core: 2. Of those that a mesh axis runs over, the one named last changes fastest.
Arguments:
- hidden_acts: bfloat16 [2, 10240, 4096], P('section', 'shard', 'tensor'), may hold values from -8 to 8
- out_grads: bfloat16 [2, 10240, 1024], P('section', 'shard'), may hold values from -8 to 8
- errors: float32 [2, 4, 1024, 4096], P('section', 'shard', None, 'tensor'), may hold values from -3 to 3
- factors: float32 [2, 32, 4096], P('section', None, 'tensor'), may hold values from -6 to 6
- whiten: float32 [2, 2, 32, 32], P('section'), may hold values from -1.5 to 3
- momentum: float32 [2, 1024, 4096], P('section', 'shard', 'tensor'), may hold values from -3 to 3
- master: float32 [2, 1024, 4096], P('section', 'shard', 'tensor'), may hold values from -3 to 3
- table: bfloat16 [32768, 1024], P(('shard', 'section'), 'tensor'), may hold values from -5 to 5
- touched_ids: int32 [1024], P(('shard', 'section')), may hold values from 0 to 32767, as said below
- touched_grads: bfloat16 [1024, 1024], P(('shard', 'section'), 'tensor'), may hold values from -5 to 5
Outputs:
- new_errors: float32 [2, 4, 1024, 4096], P('section', 'shard', None, 'tensor')
- new_factors: float32 [2, 32, 4096], P('section', None, 'tensor')
- new_momentum: float32 [2, 1024, 4096], P('section', 'shard', 'tensor')
- new_master: float32 [2, 1024, 4096], P('section', 'shard', 'tensor')
- new_weights: bfloat16 [2, 1024, 4096], P('section', None, 'tensor')
- new_table: bfloat16 [32768, 1024], P(('shard', 'section'), 'tensor')
The draws below stay inside these ranges and needn't reach their ends.
Inputs may be any that keep to these rules, and one draw needn't show every extreme that they name: `touched_ids`: the 128 ids of one device of shard and section name at most 32 rows in each block of 4096 vocabulary rows; in every draw one block receives exactly 32 rows from every device.
All inputs are finite; a program needn't handle non-finite values.
Results may differ from the reference program's by a relative error of at most 0.0036.
Values may be sent and summed in bfloat16 or wider, within the bound.
A program may use at most 128 MiB of HBM per device.

```python
import jax
import jax.numpy as jnp
from jax import lax

D = 1024
FF = 4096
R = 32
ROUNDS = 2
VOC_DEV = 4096
TOK_DEV = 2560
ROWS_DEV = 128
LAYERS = 2
TOKENS = 10240
OWNERS = 8
VOCAB = 32768
ROWS_ALL = 1024
CAP = 32
N_SHARD = 4


def draw_hidden_acts(key, part):
    noise_key = jax.random.fold_in(key, 0)
    column = jnp.arange(FF, dtype=jnp.float32) / FF
    col_scale = 0.5 * jnp.power(10.0, column - 0.5)
    base = jnp.clip(jax.random.normal(noise_key, (LAYERS, TOKENS, FF), jnp.float32), -4.0, 4.0)
    return (base * col_scale).astype(jnp.bfloat16)


def draw_out_grads(key, part):
    noise_key = jax.random.fold_in(jax.random.fold_in(key, 7), 0)
    column = jnp.arange(D, dtype=jnp.float32) / D
    col_scale = 0.5 * jnp.power(10.0, column - 0.5) / jnp.sqrt(jnp.float32(TOK_DEV))
    base = jnp.clip(jax.random.normal(noise_key, (LAYERS, TOKENS, D), jnp.float32), -4.0, 4.0)
    return (base * col_scale).astype(jnp.bfloat16)


def draw_whiten(key, part):
    diag_key, off_key = jax.random.split(jax.random.fold_in(key, 11))
    identity = jnp.eye(R, dtype=jnp.float32)
    diagonal = jax.random.uniform(diag_key, (LAYERS, ROUNDS, 1, R), jnp.float32, 0.7, 1.3)
    off_part = 0.25 * jnp.clip(jax.random.normal(off_key, (LAYERS, ROUNDS, R, R), jnp.float32), -4.0, 4.0)
    return identity * diagonal + off_part * (1.0 - identity)


def draw_touched_ids(key, part):
    capacity = CAP
    common_key, block_key = jax.random.split(jax.random.fold_in(key, 13))
    full_owner = jax.random.randint(common_key, (), 0, OWNERS, dtype=jnp.int32)

    def one_block(block_seed):
        slot_key, order_key, offset_key = jax.random.split(block_seed, 3)
        slot_list = jax.random.permutation(slot_key, (OWNERS - 1) * capacity).astype(jnp.int32)
        others = slot_list[:ROWS_DEV - capacity] // capacity
        others = others + (others >= full_owner).astype(jnp.int32)
        owners_of = jnp.concatenate([jnp.full((capacity,), full_owner, jnp.int32), others.astype(jnp.int32)])
        owners_of = jax.random.permutation(order_key, owners_of).astype(jnp.int32)
        offsets = jax.random.randint(offset_key, (ROWS_DEV,), 0, VOC_DEV, dtype=jnp.int32)
        return (owners_of * VOC_DEV + offsets).astype(jnp.int32)
    block_keys = jax.random.split(block_key, OWNERS)
    return jax.vmap(one_block)(block_keys).reshape(ROWS_ALL).astype(jnp.int32)


def block_levels(stream_key, shape, shards, smallest, high):
    level, own = 1.0, jax.random.fold_in(stream_key, 6)
    for dim, parts in shards:
        heights = jnp.exp(jax.random.uniform(jax.random.fold_in(own, dim), (parts,), jnp.float32, smallest / len(shards), high / len(shards)))
        level = level * jnp.repeat(heights, shape[dim] // parts).reshape([-1 if axis == dim else 1 for axis in range(len(shape))])
    return level


def scatter_about(own_key, shape, scale, most, cuts=(), kind=jnp.bfloat16):
    values = scale * jax.random.normal(own_key, shape, jnp.float32)
    if cuts:
        values = values * block_levels(own_key, shape, cuts, -0.22, 0.18)
    return jnp.clip(values, -most, most).astype(kind)


def setup_inputs(seed: int = 0) -> dict:
    key_list = jax.random.split(jax.random.key(seed), 11)
    hidden_acts = draw_hidden_acts(jax.random.fold_in(key_list[10], 71), 0)
    out_grads = draw_out_grads(jax.random.fold_in(key_list[10], 71), 0)
    errors = scatter_about(key_list[2], (LAYERS, N_SHARD, D, FF), 0.5, 3.0, ((0, 2), (1, 4), (3, 4)), jnp.float32)
    factors = scatter_about(key_list[3], (LAYERS, R, FF), 1.0, 6.0, ((0, 2), (2, 4)), jnp.float32)
    whiten = draw_whiten(jax.random.fold_in(key_list[10], 71), 0)
    momentum = scatter_about(key_list[5], (LAYERS, D, FF), 0.5, 3.0, ((0, 2), (1, 4), (2, 4)), jnp.float32)
    master = scatter_about(key_list[6], (LAYERS, D, FF), 0.5, 3.0, ((0, 2), (1, 4), (2, 4)), jnp.float32)
    table = scatter_about(key_list[7], (VOCAB, D), 1.0, 5.0, ((0, 8), (1, 4)))
    touched_ids = draw_touched_ids(jax.random.fold_in(key_list[10], 71), 0)
    touched_grads = scatter_about(key_list[9], (ROWS_ALL, D), 1.0, 5.0, ((0, 8), (1, 4)))
    return dict(hidden_acts=hidden_acts, out_grads=out_grads, errors=errors, factors=factors, whiten=whiten, momentum=momentum, master=master, table=table, touched_ids=touched_ids, touched_grads=touched_grads)


epsilon = 1e-06
momentum_decay = 0.9
learn_rate = 0.1
embed_rate = 0.25
clip_level = 0.03
highest = lax.Precision.HIGHEST

def corrected_block(pieces):
    grads_one, acts_one, error_one = pieces
    gradient = jnp.dot(grads_one.T, acts_one, preferred_element_type=jnp.float32)
    rounded = lax.optimization_barrier(gradient.astype(jnp.bfloat16))
    return rounded.astype(jnp.float32) + error_one

def reference(hidden_acts, out_grads, errors, factors, whiten, momentum, master, table, touched_ids, touched_grads):
    errors_list = []
    factor_list = []
    approx_list = []
    for which_layer in range(LAYERS):
        acts_layer = hidden_acts[which_layer].reshape(N_SHARD, TOK_DEV, FF)
        grads_layer = out_grads[which_layer].reshape(N_SHARD, TOK_DEV, D)
        corrected = lax.map(corrected_block, (grads_layer, acts_layer, errors[which_layer]))
        right_part = factors[which_layer]
        left_unit = None
        for power_round in range(ROUNDS):
            left_part = jnp.einsum('rf,ndf->rd', right_part, corrected, precision=highest)
            whitened = jnp.dot(whiten[which_layer, power_round].T, left_part, precision=highest)
            left_unit = whitened * lax.rsqrt(jnp.sum(whitened * whitened) / R + epsilon)
            right_part = jnp.einsum('rd,ndf->rf', left_unit, corrected, precision=highest) / N_SHARD
        approx = jnp.dot(left_unit.T, right_part, precision=highest)
        errors_list.append(corrected - approx[None])
        factor_list.append(right_part)
        approx_list.append(approx)
    approx_all = jnp.stack(approx_list)
    total_squares = jnp.sum(approx_all * approx_all)
    spread = jnp.sqrt(total_squares / (LAYERS * D * FF) + epsilon)
    clip_factor = jnp.minimum(1.0, clip_level / spread)
    new_momentum = momentum_decay * momentum + clip_factor * approx_all
    new_master = master - learn_rate * new_momentum
    new_weights = new_master.astype(jnp.bfloat16)
    table_grad = jnp.zeros((VOCAB, D), jnp.float32).at[touched_ids].add(touched_grads.astype(jnp.float32))
    new_table = (table.astype(jnp.float32) - embed_rate * table_grad).astype(jnp.bfloat16)
    return (jnp.stack(errors_list), jnp.stack(factor_list), new_momentum, new_master, new_weights, new_table)
```

```python
import functools

import jax
import jax.numpy as jnp
from jax import lax
from jax.experimental import pallas as pl
from jax.experimental.pallas import tpu as pltpu
from jax.sharding import PartitionSpec as P

ROUNDS = 2
LANES = 128

epsilon = 1e-06
momentum_decay = 0.9
learn_rate = 0.1
embed_rate = 0.25
clip_level = 0.03
highest = lax.Precision.HIGHEST
f32 = jnp.float32
bf16 = jnp.bfloat16
MESH = pl.DeviceIdType.MESH


def split(x):
    high = x.astype(bf16)
    low = (x - high.astype(f32)).astype(bf16)
    return high, low


def pieces(rank, width, count):
    rows = rank * (width // LANES) // count
    step = min(rows, rank)
    out = []
    for g in range(count):
        parts = []
        for at in range(0, rows, step):
            flat = g * rows + at
            parts.append((at, flat % rank, flat // rank * LANES, step))
        out.append(parts)
    return rows, out


def power_kernel(
    sizes,
    corrected_ref,
    factors_ref,
    whiten_ref,
    left_ref,
    right_ref,
    total_ref,
    high_ref,
    low_ref,
    lsend,
    lrecv,
    lgath,
    rsend,
    rrecv,
    rgath,
    square,
    full,
    lsem,
    rsem,
    qsem,
):
    shards, tensors, sections = sizes
    rank = factors_ref.shape[0]
    shard = lax.axis_index("shard")
    tensor = lax.axis_index("tensor")
    section = lax.axis_index("section")
    group = shards * tensors
    me = shard * tensors + tensor

    def left_peer(k):
        index = lax.rem(me + k, group)
        return index, {"shard": index // tensors, "tensor": lax.rem(index, tensors)}

    def right_peer(k):
        index = lax.rem(shard + k, shards)
        return index, {"shard": index}

    me_square = section * tensors + tensor
    squares = sections * tensors

    def square_peer(k):
        index = lax.rem(me_square + k, squares)
        return index, {"section": index // tensors, "tensor": lax.rem(index, tensors)}

    barrier = pltpu.get_barrier_semaphore()

    @pl.loop(1, group)
    def _(k):
        pl.semaphore_signal(barrier, inc=1, device_id=left_peer(k)[1], device_id_type=MESH)

    for other in range(1, sections):
        for t in range(tensors):
            there = {"section": lax.rem(section + other, sections), "tensor": t}
            pl.semaphore_signal(barrier, inc=1, device_id=there, device_id_type=MESH)

    high, low = split(corrected_ref[...])
    high_ref[...] = high
    low_ref[...] = low
    pl.semaphore_wait(barrier, group - 1 + (sections - 1) * tensors)

    def exchange(count, copy):
        @pl.loop(1, count)
        def _(k):
            copy(k).start()

        @pl.loop(1, count)
        def _(k):
            copy(k).wait()

    def all_reduce(value, count, own, peer, send, recv, gath, sems):
        rows, cuts = pieces(value.shape[0], value.shape[1], count)
        for g in range(count):
            for at, row, col, step in cuts[g]:
                send[g, at : at + step, :] = value[row : row + step, col : col + LANES]

        def scatter(k):
            index, there = peer(k)
            return pltpu.make_async_remote_copy(
                src_ref=send.at[index],
                dst_ref=recv.at[k],
                send_sem=sems.at[0, k],
                recv_sem=sems.at[1, k],
                device_id=there,
                device_id_type=MESH,
            )

        exchange(count, scatter)
        total = send[own]
        for k in range(1, count):
            total = total + recv[k]
        gath[own] = total

        def gather(k):
            _, there = peer(k)
            return pltpu.make_async_remote_copy(
                src_ref=gath.at[own],
                dst_ref=gath.at[own],
                send_sem=sems.at[2, k],
                recv_sem=sems.at[3, k],
                device_id=there,
                device_id_type=MESH,
            )

        exchange(count, gather)
        for g in range(count):
            for at, row, col, step in cuts[g]:
                full[row : row + step, col : col + LANES] = gath[g, at : at + step, :]
        return full[...]

    def times(x, dims):
        x_high, x_low = split(x)
        both = jnp.concatenate([x_high, x_low], axis=0)
        first = lax.dot_general(both, high_ref[...], (dims, ((), ())), preferred_element_type=f32)
        second = lax.dot_general(x_high, low_ref[...], (dims, ((), ())), preferred_element_type=f32)
        return first[:rank] + (first[rank:] + second)

    right = factors_ref[...]
    left_unit = None
    for turn in range(ROUNDS):
        left_part = times(right, ((1,), (1,)))
        left = all_reduce(
            left_part, group, me, left_peer, lsend.at[turn], lrecv.at[turn], lgath.at[turn], lsem.at[turn]
        )
        whitened = lax.dot_general(
            whiten_ref[turn], left, (((0,), (0,)), ((), ())), precision=highest, preferred_element_type=f32
        )
        left_unit = whitened * lax.rsqrt(jnp.sum(whitened * whitened) / rank + epsilon)
        right_part = times(left_unit, ((1,), (0,)))
        right = all_reduce(
            right_part, shards, shard, right_peer, rsend.at[turn], rrecv.at[turn], rgath.at[turn], rsem.at[turn]
        ) * (1.0 / shards)

    right_ref[...] = right
    last = (((1,), (1,)), ((), ()))
    gram_left = lax.dot_general(left_unit, left_unit, last, precision=highest, preferred_element_type=f32)
    gram_right = lax.dot_general(right, right, last, precision=highest, preferred_element_type=f32)
    square[0] = jnp.full(square.shape[1:], jnp.sum(gram_left * gram_right), f32)

    def share(k):
        _, there = square_peer(k)
        return pltpu.make_async_remote_copy(
            src_ref=square.at[0],
            dst_ref=square.at[k],
            send_sem=qsem.at[0, k],
            recv_sem=qsem.at[1, k],
            device_id=there,
            device_id_type=MESH,
        )

    @pl.loop(1, squares)
    def _(k):
        share(k).start()

    left_high = left_unit.astype(bf16).astype(f32)
    stacked = jnp.concatenate([left_high, left_unit - left_high, left_high], axis=0)
    left_ref[...] = stacked.T.astype(bf16)

    @pl.loop(1, squares)
    def _(k):
        share(k).wait()

    total = square[0]
    for k in range(1, squares):
        total = total + square[k]
    total_ref[...] = total


def run_power(sizes, corrected, factors, whiten):
    shards, tensors, sections = sizes
    rank, width = factors.shape
    depth = corrected.shape[0]
    group = shards * tensors
    left_rows = rank * (depth // LANES) // group
    right_rows = rank * (width // LANES) // shards
    vmem = pl.BlockSpec(memory_space=pltpu.VMEM)
    return pl.pallas_call(
        functools.partial(power_kernel, sizes),
        out_shape=(
            jax.ShapeDtypeStruct((depth, 3 * rank), bf16),
            jax.ShapeDtypeStruct((rank, width), f32),
            jax.ShapeDtypeStruct((8, LANES), f32),
        ),
        in_specs=[vmem] * 3,
        out_specs=(vmem,) * 3,
        scratch_shapes=[
            pltpu.VMEM((depth, width), bf16),
            pltpu.VMEM((depth, width), bf16),
            pltpu.VMEM((ROUNDS, group, left_rows, LANES), f32),
            pltpu.VMEM((ROUNDS, group, left_rows, LANES), f32),
            pltpu.VMEM((ROUNDS, group, left_rows, LANES), f32),
            pltpu.VMEM((ROUNDS, shards, right_rows, LANES), f32),
            pltpu.VMEM((ROUNDS, shards, right_rows, LANES), f32),
            pltpu.VMEM((ROUNDS, shards, right_rows, LANES), f32),
            pltpu.VMEM((sections * tensors, 8, LANES), f32),
            pltpu.VMEM((rank, max(depth, width)), f32),
            pltpu.SemaphoreType.DMA((ROUNDS, 4, group)),
            pltpu.SemaphoreType.DMA((ROUNDS, 4, shards)),
            pltpu.SemaphoreType.DMA((2, sections * tensors)),
        ],
        compiler_params=pltpu.CompilerParams(
            collective_id=0, has_side_effects=True, vmem_limit_bytes=40 * 2**20
        ),
        cost_estimate=pl.CostEstimate(flops=10**9, bytes_accessed=120 * 10**6, transcendentals=0),
        name="power_rounds",
    )(corrected, factors, whiten)


def update_kernel(
    entries,
    corrected_ref,
    left_ref,
    right_ref,
    total_ref,
    base_ref,
    momentum_ref,
    master_ref,
    errors_out,
    factors_out,
    momentum_out,
    master_out,
    weights_out,
):
    block = pl.program_id(0)
    right = right_ref[...]
    high, low = split(right)
    stacked = jnp.concatenate([high, high, low], axis=0)
    approx = jnp.dot(left_ref[...], stacked, preferred_element_type=f32)
    errors_out[...] = corrected_ref[...] - approx
    spread = jnp.sqrt(total_ref[0:1, 0:1] / entries + epsilon)
    clip = jnp.minimum(1.0, clip_level / spread)
    clipped = clip * approx

    @pl.when(block == 0)
    def _():
        factors_out[...] = right

    own = block == lax.axis_index("shard")

    @pl.when(own)
    def _():
        moved = momentum_decay * momentum_ref[...] + clipped
        stepped = master_ref[...] - learn_rate * moved
        momentum_out[...] = moved
        master_out[...] = stepped
        weights_out[...] = stepped.astype(bf16)

    @pl.when(jnp.logical_not(own))
    def _():
        weights_out[...] = (base_ref[...].astype(f32) - learn_rate * clipped).astype(bf16)


def run_update(shards, entries, corrected, left, right, total, base, momentum, master):
    depth, width = corrected.shape
    rank = right.shape[0]
    rows = depth // shards
    moving = lambda w: pl.BlockSpec((rows, w), lambda i: (i, 0))
    fixed = lambda shape: pl.BlockSpec(shape, lambda i: (0, 0))
    return pl.pallas_call(
        functools.partial(update_kernel, entries),
        grid=(shards,),
        out_shape=(
            jax.ShapeDtypeStruct((depth, width), f32),
            jax.ShapeDtypeStruct((rank, width), f32),
            jax.ShapeDtypeStruct((rows, width), f32),
            jax.ShapeDtypeStruct((rows, width), f32),
            jax.ShapeDtypeStruct((depth, width), bf16),
        ),
        in_specs=[
            moving(width),
            moving(left.shape[1]),
            fixed(right.shape),
            fixed(total.shape),
            moving(width),
            fixed((rows, width)),
            fixed((rows, width)),
        ],
        out_specs=(
            moving(width),
            fixed((rank, width)),
            fixed((rows, width)),
            fixed((rows, width)),
            moving(width),
        ),
        name="apply_update",
    )(corrected, left, right, total, base, momentum, master)


def table_kernel(ids_ref, rows_ref, table_ref, out_ref):
    count = table_ref.shape[0]
    first = pl.program_id(0) * count
    places = lax.broadcasted_iota(jnp.int32, (count, ids_ref.shape[1]), 0)
    hit = places == (ids_ref[...] - first)
    chosen = jnp.where(hit, 1.0, 0.0).astype(bf16)
    grad = jnp.dot(chosen, rows_ref[...], preferred_element_type=f32)
    out_ref[...] = (table_ref[...].astype(f32) - embed_rate * grad).astype(bf16)


def run_table(ids, rows, table):
    count = 512
    return pl.pallas_call(
        table_kernel,
        grid=(table.shape[0] // count,),
        out_shape=jax.ShapeDtypeStruct(table.shape, bf16),
        in_specs=[
            pl.BlockSpec(ids.shape, lambda i: (0, 0)),
            pl.BlockSpec(rows.shape, lambda i: (0, 0)),
            pl.BlockSpec((count, table.shape[1]), lambda i: (i, 0)),
        ],
        out_specs=pl.BlockSpec((count, table.shape[1]), lambda i: (i, 0)),
        name="table_update",
    )(ids, rows, table)


def solution(mesh):
    shards, tensors, sections = (mesh.shape[a] for a in ("shard", "tensor", "section"))
    sizes = (shards, tensors, sections)

    def on_device(
        hidden_acts, out_grads, errors, factors, whiten, momentum, master, table, touched_ids, touched_grads
    ):
        base_own = (master[0] - (learn_rate * momentum_decay) * momentum[0]).astype(bf16)
        base = lax.all_gather(base_own, "shard", axis=0, tiled=True)
        rows = lax.all_gather(touched_grads, ("shard", "section"), axis=0, tiled=True)
        ids = lax.all_gather(touched_ids, ("shard", "section"), axis=0, tiled=True)
        grad = lax.dot_general(
            out_grads[0], hidden_acts[0], (((0,), (0,)), ((), ())), preferred_element_type=f32
        )
        rounded = lax.optimization_barrier(grad.astype(bf16))
        corrected = rounded.astype(f32) + errors[0, 0]
        left, right, total = run_power(sizes, corrected, factors[0], whiten[0])
        entries = sections * corrected.shape[0] * corrected.shape[1] * tensors
        new_errors, new_factors, new_momentum, new_master, new_weights = run_update(
            shards, entries, corrected, left, right, total, base, momentum[0], master[0]
        )
        first_row = lax.axis_index(("shard", "section")) * table.shape[0]
        new_table = run_table((ids - first_row)[None], rows, table)
        return (
            new_errors[None, None],
            new_factors[None],
            new_momentum[None],
            new_master[None],
            new_weights[None],
            new_table,
        )

    in_specs = (
        P("section", "shard", "tensor"),
        P("section", "shard", None),
        P("section", "shard", None, "tensor"),
        P("section", None, "tensor"),
        P("section", None, None, None),
        P("section", "shard", "tensor"),
        P("section", "shard", "tensor"),
        P(("shard", "section"), "tensor"),
        P(("shard", "section")),
        P(("shard", "section"), "tensor"),
    )
    out_specs = (
        P("section", "shard", None, "tensor"),
        P("section", None, "tensor"),
        P("section", "shard", "tensor"),
        P("section", "shard", "tensor"),
        P("section", None, "tensor"),
        P(("shard", "section"), "tensor"),
    )
    return jax.shard_map(on_device, mesh=mesh, in_specs=in_specs, out_specs=out_specs, check_vma=False)
```

```python
import functools

import jax
import jax.numpy as jnp
from jax import lax
from jax.experimental import pallas as pl
from jax.experimental.pallas import tpu as pltpu
from jax.sharding import PartitionSpec as P

ROUNDS = 2
LANES = 128

epsilon = 1e-06
momentum_decay = 0.9
learn_rate = 0.1
embed_rate = 0.25
clip_level = 0.03
highest = lax.Precision.HIGHEST
f32 = jnp.float32
bf16 = jnp.bfloat16
MESH = pl.DeviceIdType.MESH


def split(x):
    high = x.astype(bf16)
    low = (x - high.astype(f32)).astype(bf16)
    return high, low


def pieces(rank, width, count):
    rows = rank * (width // LANES) // count
    step = min(rows, rank)
    out = []
    for g in range(count):
        parts = []
        for at in range(0, rows, step):
            flat = g * rows + at
            parts.append((at, flat % rank, flat // rank * LANES, step))
        out.append(parts)
    return rows, out


def pack_rows(ids, touched, vocab, packed):
    owners, cap, _ = packed.shape
    count = touched.shape[0]
    owner = ids // vocab
    place = ids - owner * vocab
    owned = lax.broadcasted_iota(jnp.int32, (owners, count), 0) == owner
    before = lax.broadcasted_iota(jnp.int32, (count, count), 0) < lax.broadcasted_iota(
        jnp.int32, (count, count), 1
    )
    one = lambda mask: jnp.where(mask, 1.0, 0.0)
    ranks = jnp.dot(one(owned).astype(bf16), one(before).astype(bf16), preferred_element_type=f32)
    rank = jnp.sum(jnp.where(owned, ranks, 0.0), axis=0, keepdims=True)
    slot = owner * cap + rank.astype(jnp.int32)
    chosen = one(lax.broadcasted_iota(jnp.int32, (owners * cap, count), 0) == slot).astype(bf16)
    line = lax.broadcasted_iota(jnp.int32, (LANES, count), 0)
    coarse, fine = place // 128, place % 128
    notes = jnp.where(line == 0, coarse, jnp.where(line == 1, fine, jnp.where(line == 2, 1, 0)))
    sent = jnp.dot(chosen, touched, preferred_element_type=f32)
    sent_notes = jnp.dot(chosen, notes.astype(f32).T.astype(bf16), preferred_element_type=f32)
    width = touched.shape[1]
    for b in range(owners):
        packed[b, :, :width] = sent[b * cap : (b + 1) * cap].astype(bf16)
        packed[b, :, width:] = sent_notes[b * cap : (b + 1) * cap].astype(bf16)


def power_kernel(
    sizes,
    vocab,
    grad_ref,
    errors_ref,
    factors_ref,
    whiten_ref,
    ids_ref,
    touched_ref,
    left_ref,
    right_ref,
    total_ref,
    found_ref,
    high_ref,
    low_ref,
    lsend,
    lrecv,
    lgath,
    rsend,
    rrecv,
    rgath,
    square,
    full,
    packed,
    found,
    lsem,
    rsem,
    qsem,
    tsem,
):
    shards, tensors, sections = sizes
    rank = factors_ref.shape[0]
    shard = lax.axis_index("shard")
    tensor = lax.axis_index("tensor")
    section = lax.axis_index("section")
    group = shards * tensors
    me = shard * tensors + tensor

    def left_peer(k):
        index = lax.rem(me + k, group)
        return index, {"shard": index // tensors, "tensor": lax.rem(index, tensors)}

    def right_peer(k):
        index = lax.rem(shard + k, shards)
        return index, {"shard": index}

    me_square = section * tensors + tensor
    squares = sections * tensors

    def square_peer(k):
        index = lax.rem(me_square + k, squares)
        return index, {"section": index // tensors, "tensor": lax.rem(index, tensors)}

    barrier = pltpu.get_barrier_semaphore()

    @pl.loop(1, group)
    def _(k):
        pl.semaphore_signal(barrier, inc=1, device_id=left_peer(k)[1], device_id_type=MESH)

    for other in range(1, sections):
        for t in range(tensors):
            there = {"section": lax.rem(section + other, sections), "tensor": t}
            pl.semaphore_signal(barrier, inc=1, device_id=there, device_id_type=MESH)

    for other in range(1, sections):
        for z in range(shards):
            there = {"section": lax.rem(section + other, sections), "shard": z}
            pl.semaphore_signal(barrier, inc=1, device_id=there, device_id_type=MESH)

    owners, cap, _ = packed.shape
    pack_rows(ids_ref[...], touched_ref[...], vocab, packed)
    block = shard * sections + section
    pl.semaphore_wait(barrier, group - 1 + (sections - 1) * (tensors + shards))

    def deliver(k):
        index = lax.rem(block + k, owners)
        return pltpu.make_async_remote_copy(
            src_ref=packed.at[index],
            dst_ref=found.at[block],
            send_sem=tsem.at[0, k],
            recv_sem=tsem.at[1, k],
            device_id={"shard": index // sections, "section": lax.rem(index, sections)},
            device_id_type=MESH,
        )

    @pl.loop(1, owners)
    def _(k):
        deliver(k).start()

    high, low = split(grad_ref[...].astype(f32) + errors_ref[...])
    high_ref[...] = high
    low_ref[...] = low

    def exchange(count, copy):
        @pl.loop(1, count)
        def _(k):
            copy(k).start()

        @pl.loop(1, count)
        def _(k):
            copy(k).wait()

    def all_reduce(value, count, own, peer, send, recv, gath, sems):
        rows, cuts = pieces(value.shape[0], value.shape[1], count)
        for g in range(count):
            for at, row, col, step in cuts[g]:
                send[g, at : at + step, :] = value[row : row + step, col : col + LANES]

        def scatter(k):
            index, there = peer(k)
            return pltpu.make_async_remote_copy(
                src_ref=send.at[index],
                dst_ref=recv.at[k],
                send_sem=sems.at[0, k],
                recv_sem=sems.at[1, k],
                device_id=there,
                device_id_type=MESH,
            )

        exchange(count, scatter)
        total = send[own]
        for k in range(1, count):
            total = total + recv[k]
        gath[own] = total

        def gather(k):
            _, there = peer(k)
            return pltpu.make_async_remote_copy(
                src_ref=gath.at[own],
                dst_ref=gath.at[own],
                send_sem=sems.at[2, k],
                recv_sem=sems.at[3, k],
                device_id=there,
                device_id_type=MESH,
            )

        exchange(count, gather)
        for g in range(count):
            for at, row, col, step in cuts[g]:
                full[row : row + step, col : col + LANES] = gath[g, at : at + step, :]
        return full[...]

    def times(x, dims):
        x_high, x_low = split(x)
        both = jnp.concatenate([x_high, x_low], axis=0)
        first = lax.dot_general(both, high_ref[...], (dims, ((), ())), preferred_element_type=f32)
        second = lax.dot_general(x_high, low_ref[...], (dims, ((), ())), preferred_element_type=f32)
        return first[:rank] + (first[rank:] + second)

    right = factors_ref[...]
    left_unit = None
    for turn in range(ROUNDS):
        left_part = times(right, ((1,), (1,)))
        left = all_reduce(
            left_part, group, me, left_peer, lsend.at[turn], lrecv.at[turn], lgath.at[turn], lsem.at[turn]
        )
        whitened = lax.dot_general(
            whiten_ref[turn], left, (((0,), (0,)), ((), ())), precision=highest, preferred_element_type=f32
        )
        left_unit = whitened * lax.rsqrt(jnp.sum(whitened * whitened) / rank + epsilon)
        right_part = times(left_unit, ((1,), (0,)))
        right = all_reduce(
            right_part, shards, shard, right_peer, rsend.at[turn], rrecv.at[turn], rgath.at[turn], rsem.at[turn]
        ) * (1.0 / shards)

    right_ref[...] = right
    last = (((1,), (1,)), ((), ()))
    gram_left = lax.dot_general(left_unit, left_unit, last, precision=highest, preferred_element_type=f32)
    gram_right = lax.dot_general(right, right, last, precision=highest, preferred_element_type=f32)
    square[0] = jnp.full(square.shape[1:], jnp.sum(gram_left * gram_right), f32)

    def share(k):
        _, there = square_peer(k)
        return pltpu.make_async_remote_copy(
            src_ref=square.at[0],
            dst_ref=square.at[k],
            send_sem=qsem.at[0, k],
            recv_sem=qsem.at[1, k],
            device_id=there,
            device_id_type=MESH,
        )

    @pl.loop(1, squares)
    def _(k):
        share(k).start()

    left_high = left_unit.astype(bf16).astype(f32)
    stacked = jnp.concatenate([left_high, left_unit - left_high, left_high], axis=0)
    left_ref[...] = stacked.T.astype(bf16)

    @pl.loop(1, squares)
    def _(k):
        share(k).wait()

    total = square[0]
    for k in range(1, squares):
        total = total + square[k]
    total_ref[...] = total

    @pl.loop(1, owners)
    def _(k):
        deliver(k).wait()

    found[block] = packed[block]
    found_ref[...] = found[...]


def run_power(sizes, vocab, grad, errors, factors, whiten, ids, touched):
    shards, tensors, sections = sizes
    rank, width = factors.shape
    depth = grad.shape[0]
    owners = shards * sections
    cap = 2 * touched.shape[0] // owners
    packed = (owners, cap, touched.shape[1] + LANES)
    group = shards * tensors
    left_rows = rank * (depth // LANES) // group
    right_rows = rank * (width // LANES) // shards
    vmem = pl.BlockSpec(memory_space=pltpu.VMEM)
    return pl.pallas_call(
        functools.partial(power_kernel, sizes, vocab),
        out_shape=(
            jax.ShapeDtypeStruct((depth, 3 * rank), bf16),
            jax.ShapeDtypeStruct((rank, width), f32),
            jax.ShapeDtypeStruct((8, LANES), f32),
            jax.ShapeDtypeStruct(packed, bf16),
        ),
        in_specs=[vmem] * 6,
        out_specs=(vmem,) * 4,
        scratch_shapes=[
            pltpu.VMEM((depth, width), bf16),
            pltpu.VMEM((depth, width), bf16),
            pltpu.VMEM((ROUNDS, group, left_rows, LANES), f32),
            pltpu.VMEM((ROUNDS, group, left_rows, LANES), f32),
            pltpu.VMEM((ROUNDS, group, left_rows, LANES), f32),
            pltpu.VMEM((ROUNDS, shards, right_rows, LANES), f32),
            pltpu.VMEM((ROUNDS, shards, right_rows, LANES), f32),
            pltpu.VMEM((ROUNDS, shards, right_rows, LANES), f32),
            pltpu.VMEM((sections * tensors, 8, LANES), f32),
            pltpu.VMEM((rank, max(depth, width)), f32),
            pltpu.VMEM(packed, bf16),
            pltpu.VMEM(packed, bf16),
            pltpu.SemaphoreType.DMA((ROUNDS, 4, group)),
            pltpu.SemaphoreType.DMA((ROUNDS, 4, shards)),
            pltpu.SemaphoreType.DMA((2, sections * tensors)),
            pltpu.SemaphoreType.DMA((2, owners)),
        ],
        compiler_params=pltpu.CompilerParams(
            collective_id=0, has_side_effects=True, vmem_limit_bytes=40 * 2**20
        ),
        cost_estimate=pl.CostEstimate(flops=10**9, bytes_accessed=120 * 10**6, transcendentals=0),
        name="power_rounds",
    )(grad, errors, factors, whiten, ids, touched)


def update_kernel(
    entries,
    grad_ref,
    errors_ref,
    left_ref,
    right_ref,
    total_ref,
    base_ref,
    momentum_ref,
    master_ref,
    errors_out,
    factors_out,
    momentum_out,
    master_out,
    weights_out,
):
    block = pl.program_id(0)
    right = right_ref[...]
    high, low = split(right)
    stacked = jnp.concatenate([high, high, low], axis=0)
    approx = jnp.dot(left_ref[...], stacked, preferred_element_type=f32)
    errors_out[...] = (grad_ref[...].astype(f32) + errors_ref[...]) - approx
    spread = jnp.sqrt(total_ref[0:1, 0:1] / entries + epsilon)
    clip = jnp.minimum(1.0, clip_level / spread)
    clipped = clip * approx

    @pl.when(block == 0)
    def _():
        factors_out[...] = right

    own = block == lax.axis_index("shard")

    @pl.when(own)
    def _():
        moved = momentum_decay * momentum_ref[...] + clipped
        stepped = master_ref[...] - learn_rate * moved
        momentum_out[...] = moved
        master_out[...] = stepped
        weights_out[...] = stepped.astype(bf16)

    @pl.when(jnp.logical_not(own))
    def _():
        weights_out[...] = (base_ref[...].astype(f32) - learn_rate * clipped).astype(bf16)


def run_update(shards, entries, grad, errors, left, right, total, base, momentum, master):
    depth, width = errors.shape
    rank = right.shape[0]
    rows = depth // shards
    moving = lambda w: pl.BlockSpec((rows, w), lambda i: (i, 0))
    fixed = lambda shape: pl.BlockSpec(shape, lambda i: (0, 0))
    return pl.pallas_call(
        functools.partial(update_kernel, entries),
        grid=(shards,),
        out_shape=(
            jax.ShapeDtypeStruct((depth, width), f32),
            jax.ShapeDtypeStruct((rank, width), f32),
            jax.ShapeDtypeStruct((rows, width), f32),
            jax.ShapeDtypeStruct((rows, width), f32),
            jax.ShapeDtypeStruct((depth, width), bf16),
        ),
        in_specs=[
            moving(width),
            moving(width),
            moving(left.shape[1]),
            fixed(right.shape),
            fixed(total.shape),
            moving(width),
            fixed((rows, width)),
            fixed((rows, width)),
        ],
        out_specs=(
            moving(width),
            fixed((rank, width)),
            fixed((rows, width)),
            fixed((rows, width)),
            moving(width),
        ),
        name="apply_update",
    )(grad, errors, left, right, total, base, momentum, master)


def table_kernel(found_ref, table_ref, out_ref):
    count, width = table_ref.shape
    first = pl.program_id(0) * count
    notes = found_ref[:, width:].astype(f32).T
    place = notes[0:1] * 128.0 + notes[1:2] - (1.0 - notes[2:3])
    index = place.astype(jnp.int32) - first
    places = lax.broadcasted_iota(jnp.int32, (count, index.shape[1]), 0)
    chosen = jnp.where(places == index, 1.0, 0.0).astype(bf16)
    grad = jnp.dot(chosen, found_ref[:, :width], preferred_element_type=f32)
    out_ref[...] = (table_ref[...].astype(f32) - embed_rate * grad).astype(bf16)


def run_table(found, table):
    count = 1024
    return pl.pallas_call(
        table_kernel,
        grid=(table.shape[0] // count,),
        out_shape=jax.ShapeDtypeStruct(table.shape, bf16),
        in_specs=[
            pl.BlockSpec(found.shape, lambda i: (0, 0)),
            pl.BlockSpec((count, table.shape[1]), lambda i: (i, 0)),
        ],
        out_specs=pl.BlockSpec((count, table.shape[1]), lambda i: (i, 0)),
        name="table_update",
    )(found, table)


def solution(mesh):
    shards, tensors, sections = (mesh.shape[a] for a in ("shard", "tensor", "section"))
    sizes = (shards, tensors, sections)

    def on_device(
        hidden_acts, out_grads, errors, factors, whiten, momentum, master, table, touched_ids, touched_grads
    ):
        base_own = (master[0] - (learn_rate * momentum_decay) * momentum[0]).astype(bf16)
        base = lax.all_gather(base_own, "shard", axis=0, tiled=True)
        grad = lax.dot_general(
            out_grads[0], hidden_acts[0], (((0,), (0,)), ((), ())), preferred_element_type=f32
        )
        rounded = grad.astype(bf16)
        left, right, total, found = run_power(
            sizes, table.shape[0], rounded, errors[0, 0], factors[0], whiten[0], touched_ids[None], touched_grads
        )
        entries = sections * rounded.shape[0] * rounded.shape[1] * tensors
        new_errors, new_factors, new_momentum, new_master, new_weights = run_update(
            shards, entries, rounded, errors[0, 0], left, right, total, base, momentum[0], master[0]
        )
        new_table = run_table(found.reshape(-1, found.shape[2]), table)
        return (
            new_errors[None, None],
            new_factors[None],
            new_momentum[None],
            new_master[None],
            new_weights[None],
            new_table,
        )

    in_specs = (
        P("section", "shard", "tensor"),
        P("section", "shard", None),
        P("section", "shard", None, "tensor"),
        P("section", None, "tensor"),
        P("section", None, None, None),
        P("section", "shard", "tensor"),
        P("section", "shard", "tensor"),
        P(("shard", "section"), "tensor"),
        P(("shard", "section")),
        P(("shard", "section"), "tensor"),
    )
    out_specs = (
        P("section", "shard", None, "tensor"),
        P("section", None, "tensor"),
        P("section", "shard", "tensor"),
        P("section", "shard", "tensor"),
        P("section", None, "tensor"),
        P(("shard", "section"), "tensor"),
    )
    return jax.shard_map(on_device, mesh=mesh, in_specs=in_specs, out_specs=out_specs, check_vma=False)
```

```python
import functools

import jax
import jax.numpy as jnp
from jax import lax
from jax.experimental import pallas as pl
from jax.experimental.pallas import tpu as pltpu
from jax.sharding import PartitionSpec as P

ROUNDS = 2
LANES = 128

epsilon = 1e-06
momentum_decay = 0.9
learn_rate = 0.1
embed_rate = 0.25
clip_level = 0.03
highest = lax.Precision.HIGHEST
f32 = jnp.float32
bf16 = jnp.bfloat16
MESH = pl.DeviceIdType.MESH


def split(x):
    high = x.astype(bf16)
    low = (x - high.astype(f32)).astype(bf16)
    return high, low


def pieces(rank, width, count):
    rows = rank * (width // LANES) // count
    step = min(rows, rank)
    out = []
    for g in range(count):
        parts = []
        for at in range(0, rows, step):
            flat = g * rows + at
            parts.append((at, flat % rank, flat // rank * LANES, step))
        out.append(parts)
    return rows, out


def pack_rows(ids, touched, vocab, packed):
    owners, cap, _ = packed.shape
    count = touched.shape[0]
    owner = ids // vocab
    place = ids - owner * vocab
    owned = lax.broadcasted_iota(jnp.int32, (owners, count), 0) == owner
    before = lax.broadcasted_iota(jnp.int32, (count, count), 0) < lax.broadcasted_iota(
        jnp.int32, (count, count), 1
    )
    one = lambda mask: jnp.where(mask, 1.0, 0.0)
    ranks = jnp.dot(one(owned).astype(bf16), one(before).astype(bf16), preferred_element_type=f32)
    rank = jnp.sum(jnp.where(owned, ranks, 0.0), axis=0, keepdims=True)
    slot = owner * cap + rank.astype(jnp.int32)
    chosen = one(lax.broadcasted_iota(jnp.int32, (owners * cap, count), 0) == slot).astype(bf16)
    line = lax.broadcasted_iota(jnp.int32, (LANES, count), 0)
    coarse, fine = place // 128, place % 128
    notes = jnp.where(line == 0, coarse, jnp.where(line == 1, fine, jnp.where(line == 2, 1, 0)))
    sent = jnp.dot(chosen, touched, preferred_element_type=f32)
    sent_notes = jnp.dot(chosen, notes.astype(f32).T.astype(bf16), preferred_element_type=f32)
    width = touched.shape[1]
    for b in range(owners):
        packed[b, :, :width] = sent[b * cap : (b + 1) * cap].astype(bf16)
        packed[b, :, width:] = sent_notes[b * cap : (b + 1) * cap].astype(bf16)


def power_kernel(
    sizes,
    vocab,
    grad_ref,
    errors_ref,
    factors_ref,
    whiten_ref,
    ids_ref,
    touched_ref,
    momentum_ref,
    master_ref,
    left_ref,
    right_ref,
    total_ref,
    found_ref,
    base_ref,
    high_ref,
    low_ref,
    lsend,
    lrecv,
    lgath,
    rsend,
    rrecv,
    rgath,
    square,
    full,
    packed,
    found,
    lsem,
    rsem,
    qsem,
    base_own,
    tsem,
    bsem,
):
    shards, tensors, sections = sizes
    rank = factors_ref.shape[0]
    shard = lax.axis_index("shard")
    tensor = lax.axis_index("tensor")
    section = lax.axis_index("section")
    group = shards * tensors
    me = shard * tensors + tensor

    def left_peer(k):
        index = lax.rem(me + k, group)
        return index, {"shard": index // tensors, "tensor": lax.rem(index, tensors)}

    def right_peer(k):
        index = lax.rem(shard + k, shards)
        return index, {"shard": index}

    me_square = section * tensors + tensor
    squares = sections * tensors

    def square_peer(k):
        index = lax.rem(me_square + k, squares)
        return index, {"section": index // tensors, "tensor": lax.rem(index, tensors)}

    barrier = pltpu.get_barrier_semaphore()

    @pl.loop(1, group)
    def _(k):
        pl.semaphore_signal(barrier, inc=1, device_id=left_peer(k)[1], device_id_type=MESH)

    for other in range(1, sections):
        for t in range(tensors):
            there = {"section": lax.rem(section + other, sections), "tensor": t}
            pl.semaphore_signal(barrier, inc=1, device_id=there, device_id_type=MESH)

    for other in range(1, sections):
        for z in range(shards):
            there = {"section": lax.rem(section + other, sections), "shard": z}
            pl.semaphore_signal(barrier, inc=1, device_id=there, device_id_type=MESH)

    base_own[...] = (master_ref[...] - (learn_rate * momentum_decay) * momentum_ref[...]).astype(bf16)
    owners, cap, _ = packed.shape
    pack_rows(ids_ref[...], touched_ref[...], vocab, packed)
    block = shard * sections + section
    pl.semaphore_wait(barrier, group - 1 + (sections - 1) * (tensors + shards))

    def deliver(k):
        index = lax.rem(block + k, owners)
        return pltpu.make_async_remote_copy(
            src_ref=packed.at[index],
            dst_ref=found.at[block],
            send_sem=tsem.at[0, k],
            recv_sem=tsem.at[1, k],
            device_id={"shard": index // sections, "section": lax.rem(index, sections)},
            device_id_type=MESH,
        )

    @pl.loop(1, owners)
    def _(k):
        deliver(k).start()

    def carry(way, step, receiving=False):
        sign = 1 if way == 0 else -1
        at = shard - sign if receiving else shard
        index = lax.rem(at - sign * step + 2 * shards, shards)
        return pltpu.make_async_remote_copy(
            src_ref=base_own if step == 0 and not receiving else base_ref.at[index],
            dst_ref=base_ref.at[index],
            send_sem=bsem.at[way, 0, step],
            recv_sem=bsem.at[way, 1, step],
            device_id={"shard": lax.rem(shard + sign + shards, shards)},
            device_id_type=MESH,
        )

    def sends(way, step):
        if way == 0:
            return jnp.logical_and(shard >= step, shard < shards - 1)
        return jnp.logical_and(shard < shards - step, shard > 0)

    def advance(step):
        for way in (0, 1):
            if step > 0:
                arrives = shard >= step if way == 0 else shard < shards - step

                @pl.when(arrives)
                def _():
                    carry(way, step - 1, True).wait_recv()

            if step < shards - 1:

                @pl.when(sends(way, step))
                def _():
                    carry(way, step).start()

    advance(0)
    high, low = split(grad_ref[...].astype(f32) + errors_ref[...])
    high_ref[...] = high
    low_ref[...] = low

    def exchange(count, copy):
        @pl.loop(1, count)
        def _(k):
            copy(k).start()

        @pl.loop(1, count)
        def _(k):
            copy(k).wait()

    def all_reduce(value, count, own, peer, send, recv, gath, sems):
        rows, cuts = pieces(value.shape[0], value.shape[1], count)
        for g in range(count):
            for at, row, col, step in cuts[g]:
                send[g, at : at + step, :] = value[row : row + step, col : col + LANES]

        def scatter(k):
            index, there = peer(k)
            return pltpu.make_async_remote_copy(
                src_ref=send.at[index],
                dst_ref=recv.at[k],
                send_sem=sems.at[0, k],
                recv_sem=sems.at[1, k],
                device_id=there,
                device_id_type=MESH,
            )

        exchange(count, scatter)
        total = send[own]
        for k in range(1, count):
            total = total + recv[k]
        gath[own] = total

        def gather(k):
            _, there = peer(k)
            return pltpu.make_async_remote_copy(
                src_ref=gath.at[own],
                dst_ref=gath.at[own],
                send_sem=sems.at[2, k],
                recv_sem=sems.at[3, k],
                device_id=there,
                device_id_type=MESH,
            )

        exchange(count, gather)
        for g in range(count):
            for at, row, col, step in cuts[g]:
                full[row : row + step, col : col + LANES] = gath[g, at : at + step, :]
        return full[...]

    def times(x, dims):
        x_high, x_low = split(x)
        both = jnp.concatenate([x_high, x_low], axis=0)
        first = lax.dot_general(both, high_ref[...], (dims, ((), ())), preferred_element_type=f32)
        second = lax.dot_general(x_high, low_ref[...], (dims, ((), ())), preferred_element_type=f32)
        return first[:rank] + (first[rank:] + second)

    right = factors_ref[...]
    left_unit = None
    for turn in range(ROUNDS):
        if 0 < 2 * turn < shards - 1:
            advance(2 * turn)
        left_part = times(right, ((1,), (1,)))
        left = all_reduce(
            left_part, group, me, left_peer, lsend.at[turn], lrecv.at[turn], lgath.at[turn], lsem.at[turn]
        )
        whitened = lax.dot_general(
            whiten_ref[turn], left, (((0,), (0,)), ((), ())), precision=highest, preferred_element_type=f32
        )
        left_unit = whitened * lax.rsqrt(jnp.sum(whitened * whitened) / rank + epsilon)
        if 2 * turn + 1 < shards - 1:
            advance(2 * turn + 1)
        right_part = times(left_unit, ((1,), (0,)))
        right = all_reduce(
            right_part, shards, shard, right_peer, rsend.at[turn], rrecv.at[turn], rgath.at[turn], rsem.at[turn]
        ) * (1.0 / shards)

    right_ref[...] = right
    last = (((1,), (1,)), ((), ()))
    gram_left = lax.dot_general(left_unit, left_unit, last, precision=highest, preferred_element_type=f32)
    gram_right = lax.dot_general(right, right, last, precision=highest, preferred_element_type=f32)
    square[0] = jnp.full(square.shape[1:], jnp.sum(gram_left * gram_right), f32)

    def share(k):
        _, there = square_peer(k)
        return pltpu.make_async_remote_copy(
            src_ref=square.at[0],
            dst_ref=square.at[k],
            send_sem=qsem.at[0, k],
            recv_sem=qsem.at[1, k],
            device_id=there,
            device_id_type=MESH,
        )

    @pl.loop(1, squares)
    def _(k):
        share(k).start()

    left_high = left_unit.astype(bf16).astype(f32)
    stacked = jnp.concatenate([left_high, left_unit - left_high, left_high], axis=0)
    left_ref[...] = stacked.T.astype(bf16)

    @pl.loop(1, squares)
    def _(k):
        share(k).wait()

    total = square[0]
    for k in range(1, squares):
        total = total + square[k]
    total_ref[...] = total

    @pl.loop(1, owners)
    def _(k):
        deliver(k).wait()

    for step in range(min(2 * ROUNDS, shards - 1), shards):
        advance(step)
    for step in range(shards - 1):
        for way in (0, 1):

            @pl.when(sends(way, step))
            def _():
                carry(way, step).wait_send()

    found[block] = packed[block]
    found_ref[...] = found[...]


def run_power(sizes, vocab, grad, errors, factors, whiten, ids, touched, momentum, master):
    shards, tensors, sections = sizes
    rank, width = factors.shape
    depth = grad.shape[0]
    owners = shards * sections
    cap = 2 * touched.shape[0] // owners
    packed = (owners, cap, touched.shape[1] + LANES)
    group = shards * tensors
    left_rows = rank * (depth // LANES) // group
    right_rows = rank * (width // LANES) // shards
    vmem = pl.BlockSpec(memory_space=pltpu.VMEM)
    return pl.pallas_call(
        functools.partial(power_kernel, sizes, vocab),
        out_shape=(
            jax.ShapeDtypeStruct((depth, 3 * rank), bf16),
            jax.ShapeDtypeStruct((rank, width), f32),
            jax.ShapeDtypeStruct((8, LANES), f32),
            jax.ShapeDtypeStruct(packed, bf16),
            jax.ShapeDtypeStruct((shards,) + master.shape, bf16),
        ),
        in_specs=[vmem] * 8,
        out_specs=(vmem,) * 4 + (pl.BlockSpec(memory_space=pl.ANY),),
        scratch_shapes=[
            pltpu.VMEM((depth, width), bf16),
            pltpu.VMEM((depth, width), bf16),
            pltpu.VMEM((ROUNDS, group, left_rows, LANES), f32),
            pltpu.VMEM((ROUNDS, group, left_rows, LANES), f32),
            pltpu.VMEM((ROUNDS, group, left_rows, LANES), f32),
            pltpu.VMEM((ROUNDS, shards, right_rows, LANES), f32),
            pltpu.VMEM((ROUNDS, shards, right_rows, LANES), f32),
            pltpu.VMEM((ROUNDS, shards, right_rows, LANES), f32),
            pltpu.VMEM((sections * tensors, 8, LANES), f32),
            pltpu.VMEM((rank, max(depth, width)), f32),
            pltpu.VMEM(packed, bf16),
            pltpu.VMEM(packed, bf16),
            pltpu.SemaphoreType.DMA((ROUNDS, 4, group)),
            pltpu.SemaphoreType.DMA((ROUNDS, 4, shards)),
            pltpu.SemaphoreType.DMA((2, sections * tensors)),
            pltpu.VMEM(master.shape, bf16),
            pltpu.SemaphoreType.DMA((2, owners)),
            pltpu.SemaphoreType.DMA((2, 2, shards)),
        ],
        compiler_params=pltpu.CompilerParams(
            collective_id=0, has_side_effects=True, vmem_limit_bytes=40 * 2**20
        ),
        cost_estimate=pl.CostEstimate(flops=10**9, bytes_accessed=120 * 10**6, transcendentals=0),
        name="power_rounds",
    )(grad, errors, factors, whiten, ids, touched, momentum, master)


def update_kernel(
    entries,
    grad_ref,
    errors_ref,
    left_ref,
    right_ref,
    total_ref,
    base_ref,
    momentum_ref,
    master_ref,
    errors_out,
    factors_out,
    momentum_out,
    master_out,
    weights_out,
):
    block = pl.program_id(0)
    right = right_ref[...]
    high, low = split(right)
    stacked = jnp.concatenate([high, high, low], axis=0)
    approx = jnp.dot(left_ref[...], stacked, preferred_element_type=f32)
    errors_out[...] = (grad_ref[...].astype(f32) + errors_ref[...]) - approx
    spread = jnp.sqrt(total_ref[0:1, 0:1] / entries + epsilon)
    clip = jnp.minimum(1.0, clip_level / spread)
    clipped = clip * approx

    @pl.when(block == 0)
    def _():
        factors_out[...] = right

    rows = approx.shape[0]
    parts = momentum_ref.shape[0] // rows
    own = block // parts == lax.axis_index("shard")
    here = pl.ds(pl.multiple_of(lax.rem(block, parts) * rows, rows), rows)

    @pl.when(own)
    def _():
        moved = momentum_decay * momentum_ref[here, :] + clipped
        stepped = master_ref[here, :] - learn_rate * moved
        momentum_out[here, :] = moved
        master_out[here, :] = stepped
        weights_out[...] = stepped.astype(bf16)

    @pl.when(jnp.logical_not(own))
    def _():
        weights_out[...] = (base_ref[...].astype(f32) - learn_rate * clipped).astype(bf16)


def run_update(shards, entries, grad, errors, left, right, total, base, momentum, master):
    depth, width = errors.shape
    rank = right.shape[0]
    rows = depth // shards
    parts = 2
    moving = lambda w: pl.BlockSpec((rows // parts, w), lambda i: (i, 0))
    fixed = lambda shape: pl.BlockSpec(shape, lambda i: (0, 0))
    return pl.pallas_call(
        functools.partial(update_kernel, entries),
        grid=(shards * parts,),
        out_shape=(
            jax.ShapeDtypeStruct((depth, width), f32),
            jax.ShapeDtypeStruct((rank, width), f32),
            jax.ShapeDtypeStruct((rows, width), f32),
            jax.ShapeDtypeStruct((rows, width), f32),
            jax.ShapeDtypeStruct((depth, width), bf16),
        ),
        in_specs=[
            moving(width),
            moving(width),
            moving(left.shape[1]),
            fixed(right.shape),
            fixed(total.shape),
            moving(width),
            fixed((rows, width)),
            fixed((rows, width)),
        ],
        out_specs=(
            moving(width),
            fixed((rank, width)),
            fixed((rows, width)),
            fixed((rows, width)),
            moving(width),
        ),
        name="apply_update",
    )(grad, errors, left, right, total, base, momentum, master)


def table_kernel(found_ref, table_ref, out_ref):
    count, width = table_ref.shape
    first = pl.program_id(0) * count
    notes = found_ref[:, width:].astype(f32).T
    place = notes[0:1] * 128.0 + notes[1:2] - (1.0 - notes[2:3])
    index = place.astype(jnp.int32) - first
    places = lax.broadcasted_iota(jnp.int32, (count, index.shape[1]), 0)
    chosen = jnp.where(places == index, 1.0, 0.0).astype(bf16)
    grad = jnp.dot(chosen, found_ref[:, :width], preferred_element_type=f32)
    out_ref[...] = (table_ref[...].astype(f32) - embed_rate * grad).astype(bf16)


def run_table(found, table):
    count = 1024
    return pl.pallas_call(
        table_kernel,
        grid=(table.shape[0] // count,),
        out_shape=jax.ShapeDtypeStruct(table.shape, bf16),
        in_specs=[
            pl.BlockSpec(found.shape, lambda i: (0, 0)),
            pl.BlockSpec((count, table.shape[1]), lambda i: (i, 0)),
        ],
        out_specs=pl.BlockSpec((count, table.shape[1]), lambda i: (i, 0)),
        name="table_update",
    )(found, table)


def solution(mesh):
    shards, tensors, sections = (mesh.shape[a] for a in ("shard", "tensor", "section"))
    sizes = (shards, tensors, sections)

    def on_device(
        hidden_acts, out_grads, errors, factors, whiten, momentum, master, table, touched_ids, touched_grads
    ):
        grad = lax.dot_general(
            out_grads[0], hidden_acts[0], (((0,), (0,)), ((), ())), preferred_element_type=f32
        )
        rounded = grad.astype(bf16)
        left, right, total, found, base = run_power(
            sizes, table.shape[0], rounded, errors[0, 0], factors[0], whiten[0], touched_ids[None], touched_grads,
            momentum[0], master[0],
        )
        entries = sections * rounded.shape[0] * rounded.shape[1] * tensors
        new_errors, new_factors, new_momentum, new_master, new_weights = run_update(
            shards, entries, rounded, errors[0, 0], left, right, total, base.reshape(rounded.shape), momentum[0], master[0]
        )
        new_table = run_table(found.reshape(-1, found.shape[2]), table)
        return (
            new_errors[None, None],
            new_factors[None],
            new_momentum[None],
            new_master[None],
            new_weights[None],
            new_table,
        )

    in_specs = (
        P("section", "shard", "tensor"),
        P("section", "shard", None),
        P("section", "shard", None, "tensor"),
        P("section", None, "tensor"),
        P("section", None, None, None),
        P("section", "shard", "tensor"),
        P("section", "shard", "tensor"),
        P(("shard", "section"), "tensor"),
        P(("shard", "section")),
        P(("shard", "section"), "tensor"),
    )
    out_specs = (
        P("section", "shard", None, "tensor"),
        P("section", None, "tensor"),
        P("section", "shard", "tensor"),
        P("section", "shard", "tensor"),
        P("section", None, "tensor"),
        P(("shard", "section"), "tensor"),
    )
    return jax.shard_map(on_device, mesh=mesh, in_specs=in_specs, out_specs=out_specs, check_vma=False)
```

```python
import functools

import jax
import jax.numpy as jnp
from jax import lax
from jax.experimental import pallas as pl
from jax.experimental.pallas import tpu as pltpu
from jax.sharding import PartitionSpec as P

ROUNDS = 2
LANES = 128

epsilon = 1e-06
momentum_decay = 0.9
learn_rate = 0.1
embed_rate = 0.25
clip_level = 0.03
highest = lax.Precision.HIGHEST
f32 = jnp.float32
bf16 = jnp.bfloat16
MESH = pl.DeviceIdType.MESH


def split(x):
    high = x.astype(bf16)
    low = (x - high.astype(f32)).astype(bf16)
    return high, low


def pieces(rank, width, count):
    rows = rank * (width // LANES) // count
    step = min(rows, rank)
    out = []
    for g in range(count):
        parts = []
        for at in range(0, rows, step):
            flat = g * rows + at
            parts.append((at, flat % rank, flat // rank * LANES, step))
        out.append(parts)
    return rows, out


def pack_rows(ids, touched, vocab, packed):
    owners, cap, _ = packed.shape
    count = touched.shape[0]
    owner = ids // vocab
    place = ids - owner * vocab
    owned = lax.broadcasted_iota(jnp.int32, (owners, count), 0) == owner
    before = lax.broadcasted_iota(jnp.int32, (count, count), 0) < lax.broadcasted_iota(
        jnp.int32, (count, count), 1
    )
    one = lambda mask: jnp.where(mask, 1.0, 0.0)
    ranks = jnp.dot(one(owned).astype(bf16), one(before).astype(bf16), preferred_element_type=f32)
    rank = jnp.sum(jnp.where(owned, ranks, 0.0), axis=0, keepdims=True)
    slot = owner * cap + rank.astype(jnp.int32)
    chosen = one(lax.broadcasted_iota(jnp.int32, (owners * cap, count), 0) == slot).astype(bf16)
    line = lax.broadcasted_iota(jnp.int32, (LANES, count), 0)
    coarse, fine = place // 128, place % 128
    notes = jnp.where(line == 0, coarse, jnp.where(line == 1, fine, jnp.where(line == 2, 1, 0)))
    sent = jnp.dot(chosen, touched, preferred_element_type=f32)
    sent_notes = jnp.dot(chosen, notes.astype(f32).T.astype(bf16), preferred_element_type=f32)
    width = touched.shape[1]
    for b in range(owners):
        packed[b, :, :width] = sent[b * cap : (b + 1) * cap].astype(bf16)
        packed[b, :, width:] = sent_notes[b * cap : (b + 1) * cap].astype(bf16)


def power_kernel(
    sizes,
    vocab,
    grad_ref,
    errors_ref,
    factors_ref,
    whiten_ref,
    ids_ref,
    touched_ref,
    below_ref,
    above_ref,
    left_ref,
    right_ref,
    total_ref,
    found_ref,
    base_ref,
    high_ref,
    low_ref,
    lsend,
    lrecv,
    lgath,
    rsend,
    rrecv,
    rgath,
    square,
    full,
    packed,
    found,
    lsem,
    rsem,
    qsem,
    tsem,
    bsem,
    nsem,
):
    shards, tensors, sections = sizes
    rank = factors_ref.shape[0]
    shard = lax.axis_index("shard")
    tensor = lax.axis_index("tensor")
    section = lax.axis_index("section")
    group = shards * tensors
    me = shard * tensors + tensor

    def left_peer(k):
        index = lax.rem(me + k, group)
        return index, {"shard": index // tensors, "tensor": lax.rem(index, tensors)}

    def right_peer(k):
        index = lax.rem(shard + k, shards)
        return index, {"shard": index}

    me_square = section * tensors + tensor
    squares = sections * tensors

    def square_peer(k):
        index = lax.rem(me_square + k, squares)
        return index, {"section": index // tensors, "tensor": lax.rem(index, tensors)}

    barrier = pltpu.get_barrier_semaphore()

    @pl.loop(1, group)
    def _(k):
        pl.semaphore_signal(barrier, inc=1, device_id=left_peer(k)[1], device_id_type=MESH)

    for other in range(1, sections):
        for t in range(tensors):
            there = {"section": lax.rem(section + other, sections), "tensor": t}
            pl.semaphore_signal(barrier, inc=1, device_id=there, device_id_type=MESH)

    for other in range(1, sections):
        for z in range(shards):
            there = {"section": lax.rem(section + other, sections), "shard": z}
            pl.semaphore_signal(barrier, inc=1, device_id=there, device_id_type=MESH)

    owners, cap, _ = packed.shape
    pack_rows(ids_ref[...], touched_ref[...], vocab, packed)
    block = shard * sections + section
    pl.semaphore_wait(barrier, group - 1 + (sections - 1) * (tensors + shards))

    def deliver(k):
        index = lax.rem(block + k, owners)
        return pltpu.make_async_remote_copy(
            src_ref=packed.at[index],
            dst_ref=found.at[block],
            send_sem=tsem.at[0, k],
            recv_sem=tsem.at[1, k],
            device_id={"shard": index // sections, "section": lax.rem(index, sections)},
            device_id_type=MESH,
        )

    @pl.loop(1, owners)
    def _(k):
        deliver(k).start()

    near = (below_ref, above_ref)

    def keep(way):
        index = lax.rem(shard + (shards - 1 if way == 0 else 1), shards)
        return pltpu.make_async_copy(near[way], base_ref.at[index], nsem.at[way])

    holds = (shard > 0, shard < shards - 1)
    for way in (0, 1):

        @pl.when(holds[way])
        def _():
            keep(way).start()

    def carry(way, step, receiving=False):
        sign = 1 if way == 0 else -1
        at = shard - sign if receiving else shard
        index = lax.rem(at - sign * step + 2 * shards, shards)
        return pltpu.make_async_remote_copy(
            src_ref=near[way] if step == 1 and not receiving else base_ref.at[index],
            dst_ref=base_ref.at[index],
            send_sem=bsem.at[way, 0, step],
            recv_sem=bsem.at[way, 1, step],
            device_id={"shard": lax.rem(shard + sign + shards, shards)},
            device_id_type=MESH,
        )

    def sends(way, step):
        if way == 0:
            return jnp.logical_and(shard >= step, shard < shards - 1)
        return jnp.logical_and(shard < shards - step, shard > 0)

    def advance(step):
        for way in (0, 1):
            if step > 1:
                arrives = shard >= step if way == 0 else shard < shards - step

                @pl.when(arrives)
                def _():
                    carry(way, step - 1, True).wait_recv()

            if step < shards - 1:

                @pl.when(sends(way, step))
                def _():
                    carry(way, step).start()

    advance(1)
    high, low = split(grad_ref[...].astype(f32) + errors_ref[...])
    high_ref[...] = high
    low_ref[...] = low

    def exchange(count, copy):
        @pl.loop(1, count)
        def _(k):
            copy(k).start()

        @pl.loop(1, count)
        def _(k):
            copy(k).wait()

    def all_reduce(value, count, own, peer, send, recv, gath, sems):
        rows, cuts = pieces(value.shape[0], value.shape[1], count)
        for g in range(count):
            for at, row, col, step in cuts[g]:
                send[g, at : at + step, :] = value[row : row + step, col : col + LANES]

        def scatter(k):
            index, there = peer(k)
            return pltpu.make_async_remote_copy(
                src_ref=send.at[index],
                dst_ref=recv.at[k],
                send_sem=sems.at[0, k],
                recv_sem=sems.at[1, k],
                device_id=there,
                device_id_type=MESH,
            )

        exchange(count, scatter)
        total = send[own]
        for k in range(1, count):
            total = total + recv[k]
        gath[own] = total

        def gather(k):
            _, there = peer(k)
            return pltpu.make_async_remote_copy(
                src_ref=gath.at[own],
                dst_ref=gath.at[own],
                send_sem=sems.at[2, k],
                recv_sem=sems.at[3, k],
                device_id=there,
                device_id_type=MESH,
            )

        exchange(count, gather)
        for g in range(count):
            for at, row, col, step in cuts[g]:
                full[row : row + step, col : col + LANES] = gath[g, at : at + step, :]
        return full[...]

    def times(x, dims):
        x_high, x_low = split(x)
        both = jnp.concatenate([x_high, x_low], axis=0)
        first = lax.dot_general(both, high_ref[...], (dims, ((), ())), preferred_element_type=f32)
        second = lax.dot_general(x_high, low_ref[...], (dims, ((), ())), preferred_element_type=f32)
        return first[:rank] + (first[rank:] + second)

    right = factors_ref[...]
    left_unit = None
    for turn in range(ROUNDS):
        if turn == 1 and shards > 3:
            advance(2)
        left_part = times(right, ((1,), (1,)))
        left = all_reduce(
            left_part, group, me, left_peer, lsend.at[turn], lrecv.at[turn], lgath.at[turn], lsem.at[turn]
        )
        whitened = lax.dot_general(
            whiten_ref[turn], left, (((0,), (0,)), ((), ())), precision=highest, preferred_element_type=f32
        )
        left_unit = whitened * lax.rsqrt(jnp.sum(whitened * whitened) / rank + epsilon)
        right_part = times(left_unit, ((1,), (0,)))
        right = all_reduce(
            right_part, shards, shard, right_peer, rsend.at[turn], rrecv.at[turn], rgath.at[turn], rsem.at[turn]
        ) * (1.0 / shards)

    right_ref[...] = right
    last = (((1,), (1,)), ((), ()))
    gram_left = lax.dot_general(left_unit, left_unit, last, precision=highest, preferred_element_type=f32)
    gram_right = lax.dot_general(right, right, last, precision=highest, preferred_element_type=f32)
    square[0] = jnp.full(square.shape[1:], jnp.sum(gram_left * gram_right), f32)

    def share(k):
        _, there = square_peer(k)
        return pltpu.make_async_remote_copy(
            src_ref=square.at[0],
            dst_ref=square.at[k],
            send_sem=qsem.at[0, k],
            recv_sem=qsem.at[1, k],
            device_id=there,
            device_id_type=MESH,
        )

    @pl.loop(1, squares)
    def _(k):
        share(k).start()

    left_high = left_unit.astype(bf16).astype(f32)
    stacked = jnp.concatenate([left_high, left_unit - left_high, left_high], axis=0)
    left_ref[...] = stacked.T.astype(bf16)

    @pl.loop(1, squares)
    def _(k):
        share(k).wait()

    total = square[0]
    for k in range(1, squares):
        total = total + square[k]
    total_ref[...] = total

    @pl.loop(1, owners)
    def _(k):
        deliver(k).wait()

    for step in range(min(3, shards - 1), shards):
        advance(step)
    for way in (0, 1):

        @pl.when(holds[way])
        def _():
            keep(way).wait()

    for step in range(1, shards - 1):
        for way in (0, 1):

            @pl.when(sends(way, step))
            def _():
                carry(way, step).wait_send()

    found[block] = packed[block]
    found_ref[...] = found[...]


def run_power(sizes, vocab, grad, errors, factors, whiten, ids, touched, below, above):
    shards, tensors, sections = sizes
    rank, width = factors.shape
    depth = grad.shape[0]
    owners = shards * sections
    cap = 2 * touched.shape[0] // owners
    packed = (owners, cap, touched.shape[1] + LANES)
    group = shards * tensors
    left_rows = rank * (depth // LANES) // group
    right_rows = rank * (width // LANES) // shards
    vmem = pl.BlockSpec(memory_space=pltpu.VMEM)
    return pl.pallas_call(
        functools.partial(power_kernel, sizes, vocab),
        out_shape=(
            jax.ShapeDtypeStruct((depth, 3 * rank), bf16),
            jax.ShapeDtypeStruct((rank, width), f32),
            jax.ShapeDtypeStruct((8, LANES), f32),
            jax.ShapeDtypeStruct(packed, bf16),
            jax.ShapeDtypeStruct((shards,) + below.shape, bf16),
        ),
        in_specs=[vmem] * 8,
        out_specs=(vmem,) * 4 + (pl.BlockSpec(memory_space=pl.ANY),),
        scratch_shapes=[
            pltpu.VMEM((depth, width), bf16),
            pltpu.VMEM((depth, width), bf16),
            pltpu.VMEM((ROUNDS, group, left_rows, LANES), f32),
            pltpu.VMEM((ROUNDS, group, left_rows, LANES), f32),
            pltpu.VMEM((ROUNDS, group, left_rows, LANES), f32),
            pltpu.VMEM((ROUNDS, shards, right_rows, LANES), f32),
            pltpu.VMEM((ROUNDS, shards, right_rows, LANES), f32),
            pltpu.VMEM((ROUNDS, shards, right_rows, LANES), f32),
            pltpu.VMEM((sections * tensors, 8, LANES), f32),
            pltpu.VMEM((rank, max(depth, width)), f32),
            pltpu.VMEM(packed, bf16),
            pltpu.VMEM(packed, bf16),
            pltpu.SemaphoreType.DMA((ROUNDS, 4, group)),
            pltpu.SemaphoreType.DMA((ROUNDS, 4, shards)),
            pltpu.SemaphoreType.DMA((2, sections * tensors)),
            pltpu.SemaphoreType.DMA((2, owners)),
            pltpu.SemaphoreType.DMA((2, 2, shards)),
            pltpu.SemaphoreType.DMA((2,)),
        ],
        compiler_params=pltpu.CompilerParams(
            collective_id=0, has_side_effects=True, vmem_limit_bytes=40 * 2**20
        ),
        cost_estimate=pl.CostEstimate(flops=10**9, bytes_accessed=120 * 10**6, transcendentals=0),
        name="power_rounds",
    )(grad, errors, factors, whiten, ids, touched, below, above)


def update_kernel(
    entries,
    grad_ref,
    errors_ref,
    left_ref,
    right_ref,
    total_ref,
    base_ref,
    momentum_ref,
    master_ref,
    errors_out,
    factors_out,
    momentum_out,
    master_out,
    weights_out,
):
    block = pl.program_id(0)
    right = right_ref[...]
    high, low = split(right)
    stacked = jnp.concatenate([high, high, low], axis=0)
    approx = jnp.dot(left_ref[...], stacked, preferred_element_type=f32)
    errors_out[...] = (grad_ref[...].astype(f32) + errors_ref[...]) - approx
    spread = jnp.sqrt(total_ref[0:1, 0:1] / entries + epsilon)
    clip = jnp.minimum(1.0, clip_level / spread)
    clipped = clip * approx

    @pl.when(block == 0)
    def _():
        factors_out[...] = right

    rows = approx.shape[0]
    parts = momentum_ref.shape[0] // rows
    own = block // parts == lax.axis_index("shard")
    here = pl.ds(pl.multiple_of(lax.rem(block, parts) * rows, rows), rows)

    @pl.when(own)
    def _():
        moved = momentum_decay * momentum_ref[here, :] + clipped
        stepped = master_ref[here, :] - learn_rate * moved
        momentum_out[here, :] = moved
        master_out[here, :] = stepped
        weights_out[...] = stepped.astype(bf16)

    @pl.when(jnp.logical_not(own))
    def _():
        weights_out[...] = (base_ref[...].astype(f32) - learn_rate * clipped).astype(bf16)


def run_update(shards, entries, grad, errors, left, right, total, base, momentum, master):
    depth, width = errors.shape
    rank = right.shape[0]
    rows = depth // shards
    parts = 1
    moving = lambda w: pl.BlockSpec((rows // parts, w), lambda i: (i, 0))
    fixed = lambda shape: pl.BlockSpec(shape, lambda i: (0, 0))
    return pl.pallas_call(
        functools.partial(update_kernel, entries),
        grid=(shards * parts,),
        out_shape=(
            jax.ShapeDtypeStruct((depth, width), f32),
            jax.ShapeDtypeStruct((rank, width), f32),
            jax.ShapeDtypeStruct((rows, width), f32),
            jax.ShapeDtypeStruct((rows, width), f32),
            jax.ShapeDtypeStruct((depth, width), bf16),
        ),
        in_specs=[
            moving(width),
            moving(width),
            moving(left.shape[1]),
            fixed(right.shape),
            fixed(total.shape),
            moving(width),
            fixed((rows, width)),
            fixed((rows, width)),
        ],
        out_specs=(
            moving(width),
            fixed((rank, width)),
            fixed((rows, width)),
            fixed((rows, width)),
            moving(width),
        ),
        name="apply_update",
    )(grad, errors, left, right, total, base, momentum, master)


def table_kernel(found_ref, table_ref, out_ref):
    count, width = table_ref.shape
    first = pl.program_id(0) * count
    notes = found_ref[:, width:].astype(f32).T
    place = notes[0:1] * 128.0 + notes[1:2] - (1.0 - notes[2:3])
    index = place.astype(jnp.int32) - first
    places = lax.broadcasted_iota(jnp.int32, (count, index.shape[1]), 0)
    chosen = jnp.where(places == index, 1.0, 0.0).astype(bf16)
    grad = jnp.dot(chosen, found_ref[:, :width], preferred_element_type=f32)
    out_ref[...] = (table_ref[...].astype(f32) - embed_rate * grad).astype(bf16)


def run_table(found, table):
    count = 1024
    return pl.pallas_call(
        table_kernel,
        grid=(table.shape[0] // count,),
        out_shape=jax.ShapeDtypeStruct(table.shape, bf16),
        in_specs=[
            pl.BlockSpec(found.shape, lambda i: (0, 0)),
            pl.BlockSpec((count, table.shape[1]), lambda i: (i, 0)),
        ],
        out_specs=pl.BlockSpec((count, table.shape[1]), lambda i: (i, 0)),
        name="table_update",
    )(found, table)


def solution(mesh):
    shards, tensors, sections = (mesh.shape[a] for a in ("shard", "tensor", "section"))
    sizes = (shards, tensors, sections)

    def on_device(
        hidden_acts, out_grads, errors, factors, whiten, momentum, master, table, touched_ids, touched_grads
    ):
        base_own = (master[0] - (learn_rate * momentum_decay) * momentum[0]).astype(bf16)
        below = lax.ppermute(base_own, "shard", [(i, i + 1) for i in range(shards - 1)])
        above = lax.ppermute(base_own, "shard", [(i + 1, i) for i in range(shards - 1)])
        grad = lax.dot_general(
            out_grads[0], hidden_acts[0], (((0,), (0,)), ((), ())), preferred_element_type=f32
        )
        rounded = grad.astype(bf16)
        left, right, total, found, base = run_power(
            sizes, table.shape[0], rounded, errors[0, 0], factors[0], whiten[0], touched_ids[None], touched_grads,
            below, above,
        )
        entries = sections * rounded.shape[0] * rounded.shape[1] * tensors
        new_errors, new_factors, new_momentum, new_master, new_weights = run_update(
            shards, entries, rounded, errors[0, 0], left, right, total, base.reshape(rounded.shape), momentum[0], master[0]
        )
        new_table = run_table(found.reshape(-1, found.shape[2]), table)
        return (
            new_errors[None, None],
            new_factors[None],
            new_momentum[None],
            new_master[None],
            new_weights[None],
            new_table,
        )

    in_specs = (
        P("section", "shard", "tensor"),
        P("section", "shard", None),
        P("section", "shard", None, "tensor"),
        P("section", None, "tensor"),
        P("section", None, None, None),
        P("section", "shard", "tensor"),
        P("section", "shard", "tensor"),
        P(("shard", "section"), "tensor"),
        P(("shard", "section")),
        P(("shard", "section"), "tensor"),
    )
    out_specs = (
        P("section", "shard", None, "tensor"),
        P("section", None, "tensor"),
        P("section", "shard", "tensor"),
        P("section", "shard", "tensor"),
        P("section", None, "tensor"),
        P(("shard", "section"), "tensor"),
    )
    return jax.shard_map(on_device, mesh=mesh, in_specs=in_specs, out_specs=out_specs, check_vma=False)
```

```python
import functools

import jax
import jax.numpy as jnp
from jax import lax
from jax.experimental import pallas as pl
from jax.experimental.pallas import tpu as pltpu
from jax.sharding import PartitionSpec as P

ROUNDS = 2
LANES = 128

epsilon = 1e-06
momentum_decay = 0.9
learn_rate = 0.1
embed_rate = 0.25
clip_level = 0.03
highest = lax.Precision.HIGHEST
f32 = jnp.float32
bf16 = jnp.bfloat16
MESH = pl.DeviceIdType.MESH


def split(x):
    high = x.astype(bf16)
    low = (x - high.astype(f32)).astype(bf16)
    return high, low


def pieces(rank, width, count):
    rows = rank * (width // LANES) // count
    step = min(rows, rank)
    out = []
    for g in range(count):
        parts = []
        for at in range(0, rows, step):
            flat = g * rows + at
            parts.append((at, flat % rank, flat // rank * LANES, step))
        out.append(parts)
    return rows, out


def pack_rows(ids, touched, vocab, packed):
    owners, cap, _ = packed.shape
    count = touched.shape[0]
    owner = ids // vocab
    place = ids - owner * vocab
    owned = lax.broadcasted_iota(jnp.int32, (owners, count), 0) == owner
    before = lax.broadcasted_iota(jnp.int32, (count, count), 0) < lax.broadcasted_iota(
        jnp.int32, (count, count), 1
    )
    one = lambda mask: jnp.where(mask, 1.0, 0.0)
    ranks = jnp.dot(one(owned).astype(bf16), one(before).astype(bf16), preferred_element_type=f32)
    rank = jnp.sum(jnp.where(owned, ranks, 0.0), axis=0, keepdims=True)
    slot = owner * cap + rank.astype(jnp.int32)
    chosen = one(lax.broadcasted_iota(jnp.int32, (owners * cap, count), 0) == slot).astype(bf16)
    line = lax.broadcasted_iota(jnp.int32, (LANES, count), 0)
    coarse, fine = place // 128, place % 128
    notes = jnp.where(line == 0, coarse, jnp.where(line == 1, fine, jnp.where(line == 2, 1, 0)))
    sent = jnp.dot(chosen, touched, preferred_element_type=f32)
    sent_notes = jnp.dot(chosen, notes.astype(f32).T.astype(bf16), preferred_element_type=f32)
    width = touched.shape[1]
    for b in range(owners):
        packed[b, :, :width] = sent[b * cap : (b + 1) * cap].astype(bf16)
        packed[b, :, width:] = sent_notes[b * cap : (b + 1) * cap].astype(bf16)


def power_kernel(
    sizes,
    vocab,
    grad_ref,
    errors_ref,
    factors_ref,
    whiten_ref,
    ids_ref,
    touched_ref,
    below_ref,
    above_ref,
    left_ref,
    right_ref,
    total_ref,
    found_ref,
    base_ref,
    high_ref,
    low_ref,
    lsend,
    lrecv,
    lgath,
    rsend,
    rrecv,
    rgath,
    square,
    full,
    packed,
    found,
    lsem,
    rsem,
    qsem,
    tsem,
    bsem,
    nsem,
):
    shards, tensors, sections = sizes
    rank = factors_ref.shape[0]
    shard = lax.axis_index("shard")
    tensor = lax.axis_index("tensor")
    section = lax.axis_index("section")
    group = shards * tensors
    me = shard * tensors + tensor

    def left_peer(k):
        index = lax.rem(me + k, group)
        return index, {"shard": index // tensors, "tensor": lax.rem(index, tensors)}

    def right_peer(k):
        index = lax.rem(shard + k, shards)
        return index, {"shard": index}

    me_square = section * tensors + tensor
    squares = sections * tensors

    def square_peer(k):
        index = lax.rem(me_square + k, squares)
        return index, {"section": index // tensors, "tensor": lax.rem(index, tensors)}

    barrier = pltpu.get_barrier_semaphore()

    @pl.loop(1, group)
    def _(k):
        pl.semaphore_signal(barrier, inc=1, device_id=left_peer(k)[1], device_id_type=MESH)

    for other in range(1, sections):
        for t in range(tensors):
            there = {"section": lax.rem(section + other, sections), "tensor": t}
            pl.semaphore_signal(barrier, inc=1, device_id=there, device_id_type=MESH)

    for other in range(1, sections):
        for z in range(shards):
            there = {"section": lax.rem(section + other, sections), "shard": z}
            pl.semaphore_signal(barrier, inc=1, device_id=there, device_id_type=MESH)

    owners, cap, _ = packed.shape
    pack_rows(ids_ref[...], touched_ref[...], vocab, packed)
    block = shard * sections + section
    pl.semaphore_wait(barrier, group - 1 + (sections - 1) * (tensors + shards))

    def deliver(k):
        index = lax.rem(block + k, owners)
        return pltpu.make_async_remote_copy(
            src_ref=packed.at[index],
            dst_ref=found.at[block],
            send_sem=tsem.at[0, k],
            recv_sem=tsem.at[1, k],
            device_id={"shard": index // sections, "section": lax.rem(index, sections)},
            device_id_type=MESH,
        )

    @pl.loop(1, owners)
    def _(k):
        deliver(k).start()

    near = (below_ref, above_ref)

    def keep(way):
        index = lax.rem(shard + (shards - 1 if way == 0 else 1), shards)
        return pltpu.make_async_copy(near[way], base_ref.at[index], nsem.at[way])

    holds = (shard > 0, shard < shards - 1)
    for way in (0, 1):

        @pl.when(holds[way])
        def _():
            keep(way).start()

    def carry(way, step, receiving=False):
        sign = 1 if way == 0 else -1
        at = shard - sign if receiving else shard
        index = lax.rem(at - sign * step + 2 * shards, shards)
        return pltpu.make_async_remote_copy(
            src_ref=near[way] if step == 1 and not receiving else base_ref.at[index],
            dst_ref=base_ref.at[index],
            send_sem=bsem.at[way, 0, step],
            recv_sem=bsem.at[way, 1, step],
            device_id={"shard": lax.rem(shard + sign + shards, shards)},
            device_id_type=MESH,
        )

    def sends(way, step):
        if way == 0:
            return jnp.logical_and(shard >= step, shard < shards - 1)
        return jnp.logical_and(shard < shards - step, shard > 0)

    def advance(step):
        for way in (0, 1):
            if step > 1:
                arrives = shard >= step if way == 0 else shard < shards - step

                @pl.when(arrives)
                def _():
                    carry(way, step - 1, True).wait_recv()

            if step < shards - 1:

                @pl.when(sends(way, step))
                def _():
                    carry(way, step).start()

    advance(1)
    high, low = split(grad_ref[...].astype(f32) + errors_ref[...])
    high_ref[...] = high
    low_ref[...] = low

    def exchange(count, copy):
        if count <= 16:
            for k in range(1, count):
                copy(k).start()
        else:

            @pl.loop(1, count)
            def _(k):
                copy(k).start()

        @pl.loop(1, count)
        def _(k):
            copy(k).wait()

    def all_reduce(value, count, own, peer, send, recv, gath, sems):
        rows, cuts = pieces(value.shape[0], value.shape[1], count)
        for g in range(count):
            for at, row, col, step in cuts[g]:
                send[g, at : at + step, :] = value[row : row + step, col : col + LANES]

        def scatter(k):
            index, there = peer(k)
            return pltpu.make_async_remote_copy(
                src_ref=send.at[index],
                dst_ref=recv.at[k],
                send_sem=sems.at[0, k],
                recv_sem=sems.at[1, k],
                device_id=there,
                device_id_type=MESH,
            )

        exchange(count, scatter)
        total = send[own]
        for k in range(1, count):
            total = total + recv[k]
        gath[own] = total

        def gather(k):
            _, there = peer(k)
            return pltpu.make_async_remote_copy(
                src_ref=gath.at[own],
                dst_ref=gath.at[own],
                send_sem=sems.at[2, k],
                recv_sem=sems.at[3, k],
                device_id=there,
                device_id_type=MESH,
            )

        exchange(count, gather)
        for g in range(count):
            for at, row, col, step in cuts[g]:
                full[row : row + step, col : col + LANES] = gath[g, at : at + step, :]
        return full[...]

    def times(x, dims):
        x_high, x_low = split(x)
        both = jnp.concatenate([x_high, x_low], axis=0)
        first = lax.dot_general(both, high_ref[...], (dims, ((), ())), preferred_element_type=f32)
        second = lax.dot_general(x_high, low_ref[...], (dims, ((), ())), preferred_element_type=f32)
        return first[:rank] + (first[rank:] + second)

    right = factors_ref[...]
    left_unit = None
    for turn in range(ROUNDS):
        if turn == 1 and shards > 3:
            advance(2)
        left_part = times(right, ((1,), (1,)))
        left = all_reduce(
            left_part, group, me, left_peer, lsend.at[turn], lrecv.at[turn], lgath.at[turn], lsem.at[turn]
        )
        whitened = lax.dot_general(
            whiten_ref[turn], left, (((0,), (0,)), ((), ())), precision=highest, preferred_element_type=f32
        )
        left_unit = whitened * lax.rsqrt(jnp.sum(whitened * whitened) / rank + epsilon)
        right_part = times(left_unit, ((1,), (0,)))
        right = all_reduce(
            right_part, shards, shard, right_peer, rsend.at[turn], rrecv.at[turn], rgath.at[turn], rsem.at[turn]
        ) * (1.0 / shards)

    right_ref[...] = right
    last = (((1,), (1,)), ((), ()))
    gram_left = lax.dot_general(left_unit, left_unit, last, precision=highest, preferred_element_type=f32)
    gram_right = lax.dot_general(right, right, last, precision=highest, preferred_element_type=f32)
    square[0] = jnp.full(square.shape[1:], jnp.sum(gram_left * gram_right), f32)

    def share(k):
        _, there = square_peer(k)
        return pltpu.make_async_remote_copy(
            src_ref=square.at[0],
            dst_ref=square.at[k],
            send_sem=qsem.at[0, k],
            recv_sem=qsem.at[1, k],
            device_id=there,
            device_id_type=MESH,
        )

    @pl.loop(1, squares)
    def _(k):
        share(k).start()

    left_high = left_unit.astype(bf16).astype(f32)
    stacked = jnp.concatenate([left_high, left_unit - left_high, left_high], axis=0)
    left_ref[...] = stacked.T.astype(bf16)

    @pl.loop(1, squares)
    def _(k):
        share(k).wait()

    total = square[0]
    for k in range(1, squares):
        total = total + square[k]
    total_ref[...] = total

    @pl.loop(1, owners)
    def _(k):
        deliver(k).wait()

    for step in range(min(3, shards - 1), shards):
        advance(step)
    for way in (0, 1):

        @pl.when(holds[way])
        def _():
            keep(way).wait()

    for step in range(1, shards - 1):
        for way in (0, 1):

            @pl.when(sends(way, step))
            def _():
                carry(way, step).wait_send()

    found[block] = packed[block]
    found_ref[...] = found[...]


def run_power(sizes, vocab, grad, errors, factors, whiten, ids, touched, below, above):
    shards, tensors, sections = sizes
    rank, width = factors.shape
    depth = grad.shape[0]
    owners = shards * sections
    cap = 2 * touched.shape[0] // owners
    packed = (owners, cap, touched.shape[1] + LANES)
    group = shards * tensors
    left_rows = rank * (depth // LANES) // group
    right_rows = rank * (width // LANES) // shards
    vmem = pl.BlockSpec(memory_space=pltpu.VMEM)
    return pl.pallas_call(
        functools.partial(power_kernel, sizes, vocab),
        out_shape=(
            jax.ShapeDtypeStruct((depth, 3 * rank), bf16),
            jax.ShapeDtypeStruct((rank, width), f32),
            jax.ShapeDtypeStruct((8, LANES), f32),
            jax.ShapeDtypeStruct(packed, bf16),
            jax.ShapeDtypeStruct((shards,) + below.shape, bf16),
        ),
        in_specs=[vmem] * 8,
        out_specs=(vmem,) * 4 + (pl.BlockSpec(memory_space=pl.ANY),),
        scratch_shapes=[
            pltpu.VMEM((depth, width), bf16),
            pltpu.VMEM((depth, width), bf16),
            pltpu.VMEM((ROUNDS, group, left_rows, LANES), f32),
            pltpu.VMEM((ROUNDS, group, left_rows, LANES), f32),
            pltpu.VMEM((ROUNDS, group, left_rows, LANES), f32),
            pltpu.VMEM((ROUNDS, shards, right_rows, LANES), f32),
            pltpu.VMEM((ROUNDS, shards, right_rows, LANES), f32),
            pltpu.VMEM((ROUNDS, shards, right_rows, LANES), f32),
            pltpu.VMEM((sections * tensors, 8, LANES), f32),
            pltpu.VMEM((rank, max(depth, width)), f32),
            pltpu.VMEM(packed, bf16),
            pltpu.VMEM(packed, bf16),
            pltpu.SemaphoreType.DMA((ROUNDS, 4, group)),
            pltpu.SemaphoreType.DMA((ROUNDS, 4, shards)),
            pltpu.SemaphoreType.DMA((2, sections * tensors)),
            pltpu.SemaphoreType.DMA((2, owners)),
            pltpu.SemaphoreType.DMA((2, 2, shards)),
            pltpu.SemaphoreType.DMA((2,)),
        ],
        compiler_params=pltpu.CompilerParams(
            collective_id=0, has_side_effects=True, vmem_limit_bytes=40 * 2**20
        ),
        cost_estimate=pl.CostEstimate(flops=10**9, bytes_accessed=120 * 10**6, transcendentals=0),
        name="power_rounds",
    )(grad, errors, factors, whiten, ids, touched, below, above)


def update_kernel(
    entries,
    grad_ref,
    errors_ref,
    left_ref,
    right_ref,
    total_ref,
    base_ref,
    momentum_ref,
    master_ref,
    errors_out,
    factors_out,
    momentum_out,
    master_out,
    weights_out,
):
    block = pl.program_id(0)
    right = right_ref[...]
    high, low = split(right)
    stacked = jnp.concatenate([high, high, low], axis=0)
    approx = jnp.dot(left_ref[...], stacked, preferred_element_type=f32)
    errors_out[...] = (grad_ref[...].astype(f32) + errors_ref[...]) - approx
    spread = jnp.sqrt(total_ref[0:1, 0:1] / entries + epsilon)
    clip = jnp.minimum(1.0, clip_level / spread)
    clipped = clip * approx

    @pl.when(block == 0)
    def _():
        factors_out[...] = right

    rows = approx.shape[0]
    parts = momentum_ref.shape[0] // rows
    own = block // parts == lax.axis_index("shard")
    here = pl.ds(pl.multiple_of(lax.rem(block, parts) * rows, rows), rows)

    @pl.when(own)
    def _():
        moved = momentum_decay * momentum_ref[here, :] + clipped
        stepped = master_ref[here, :] - learn_rate * moved
        momentum_out[here, :] = moved
        master_out[here, :] = stepped
        weights_out[...] = stepped.astype(bf16)

    @pl.when(jnp.logical_not(own))
    def _():
        weights_out[...] = (base_ref[...].astype(f32) - learn_rate * clipped).astype(bf16)


def run_update(shards, entries, grad, errors, left, right, total, base, momentum, master):
    depth, width = errors.shape
    rank = right.shape[0]
    rows = depth // shards
    parts = 1
    moving = lambda w: pl.BlockSpec((rows // parts, w), lambda i: (i, 0))
    fixed = lambda shape: pl.BlockSpec(shape, lambda i: (0, 0))
    return pl.pallas_call(
        functools.partial(update_kernel, entries),
        grid=(shards * parts,),
        out_shape=(
            jax.ShapeDtypeStruct((depth, width), f32),
            jax.ShapeDtypeStruct((rank, width), f32),
            jax.ShapeDtypeStruct((rows, width), f32),
            jax.ShapeDtypeStruct((rows, width), f32),
            jax.ShapeDtypeStruct((depth, width), bf16),
        ),
        in_specs=[
            moving(width),
            moving(width),
            moving(left.shape[1]),
            fixed(right.shape),
            fixed(total.shape),
            moving(width),
            fixed((rows, width)),
            fixed((rows, width)),
        ],
        out_specs=(
            moving(width),
            fixed((rank, width)),
            fixed((rows, width)),
            fixed((rows, width)),
            moving(width),
        ),
        name="apply_update",
    )(grad, errors, left, right, total, base, momentum, master)


def table_kernel(found_ref, table_ref, out_ref):
    count, width = table_ref.shape
    first = pl.program_id(0) * count
    notes = found_ref[:, width:].astype(f32).T
    place = notes[0:1] * 128.0 + notes[1:2] - (1.0 - notes[2:3])
    index = place.astype(jnp.int32) - first
    places = lax.broadcasted_iota(jnp.int32, (count, index.shape[1]), 0)
    chosen = jnp.where(places == index, 1.0, 0.0).astype(bf16)
    grad = jnp.dot(chosen, found_ref[:, :width], preferred_element_type=f32)
    out_ref[...] = (table_ref[...].astype(f32) - embed_rate * grad).astype(bf16)


def run_table(found, table):
    count = 1024
    return pl.pallas_call(
        table_kernel,
        grid=(table.shape[0] // count,),
        out_shape=jax.ShapeDtypeStruct(table.shape, bf16),
        in_specs=[
            pl.BlockSpec(found.shape, lambda i: (0, 0)),
            pl.BlockSpec((count, table.shape[1]), lambda i: (i, 0)),
        ],
        out_specs=pl.BlockSpec((count, table.shape[1]), lambda i: (i, 0)),
        name="table_update",
    )(found, table)


def solution(mesh):
    shards, tensors, sections = (mesh.shape[a] for a in ("shard", "tensor", "section"))
    sizes = (shards, tensors, sections)

    def on_device(
        hidden_acts, out_grads, errors, factors, whiten, momentum, master, table, touched_ids, touched_grads
    ):
        base_own = (master[0] - (learn_rate * momentum_decay) * momentum[0]).astype(bf16)
        below = lax.ppermute(base_own, "shard", [(i, i + 1) for i in range(shards - 1)])
        above = lax.ppermute(base_own, "shard", [(i + 1, i) for i in range(shards - 1)])
        grad = lax.dot_general(
            out_grads[0], hidden_acts[0], (((0,), (0,)), ((), ())), preferred_element_type=f32
        )
        rounded = grad.astype(bf16)
        left, right, total, found, base = run_power(
            sizes, table.shape[0], rounded, errors[0, 0], factors[0], whiten[0], touched_ids[None], touched_grads,
            below, above,
        )
        entries = sections * rounded.shape[0] * rounded.shape[1] * tensors
        new_errors, new_factors, new_momentum, new_master, new_weights = run_update(
            shards, entries, rounded, errors[0, 0], left, right, total, base.reshape(rounded.shape), momentum[0], master[0]
        )
        new_table = run_table(found.reshape(-1, found.shape[2]), table)
        return (
            new_errors[None, None],
            new_factors[None],
            new_momentum[None],
            new_master[None],
            new_weights[None],
            new_table,
        )

    in_specs = (
        P("section", "shard", "tensor"),
        P("section", "shard", None),
        P("section", "shard", None, "tensor"),
        P("section", None, "tensor"),
        P("section", None, None, None),
        P("section", "shard", "tensor"),
        P("section", "shard", "tensor"),
        P(("shard", "section"), "tensor"),
        P(("shard", "section")),
        P(("shard", "section"), "tensor"),
    )
    out_specs = (
        P("section", "shard", None, "tensor"),
        P("section", None, "tensor"),
        P("section", "shard", "tensor"),
        P("section", "shard", "tensor"),
        P("section", None, "tensor"),
        P(("shard", "section"), "tensor"),
    )
    return jax.shard_map(on_device, mesh=mesh, in_specs=in_specs, out_specs=out_specs, check_vma=False)
```
